32 devices in a mesh: shot: 2 (over y), gx: 4 (over z), gy: 4 (over x, core).
Axes of the slice: x: 2, y: 2, z: 4, core: 2. Of those that a mesh axis runs over, the one named last changes fastest.
Arguments:
- source_prev: float32 [64, 32, 320], P(('shot', 'gx'), 'gy'), parts along dimension 0, may hold values from -0.6 to 0.6
- source_now: float32 [64, 32, 320], P(('shot', 'gx'), 'gy'), parts along dimension 0, may hold values from -0.6 to 0.6
- receiver_prev: float32 [64, 32, 320], P(('shot', 'gx'), 'gy'), parts along dimension 0, may hold values from -6 to 6
- receiver_now: float32 [64, 32, 320], P(('shot', 'gx'), 'gy'), parts along dimension 0, may hold values from -6 to 6
- speed_squared: float32 [64, 32, 320], P(('shot', 'gx'), 'gy'), parts along dimension 0, may hold values from 0.05 to 0.18
- wavelet: float32 [20], P('shot'), parts along dimension 0, may hold values from -40 to 40
- source_cell: int32 [2], P('shot'), parts along dimension 0, may hold values from 0 to 327679
- traces: float32 [20, 1024], P('shot', ('gx', 'gy')), parts along dimension 0, may hold values from -18 to 18
- receiver_cells: int32 [2, 1024], P('shot', ('gx', 'gy')), parts along dimension 0, may hold values from 0 to 1023
- plan: int32 [8], P('shot'), parts along dimension 0, may hold values from 0 to 9, as said below
- stored_snapshots: bfloat16 [8, 32, 32, 320], P('shot', 'gx', 'gy'), parts along dimension 0, may hold values from -6 to 6
- image_before: float32 [64, 32, 320], P(('shot', 'gx'), 'gy'), parts along dimension 0, may hold values from -6 to 6
Outputs:
- new_source_prev: float32 [64, 32, 320], P(('shot', 'gx'), 'gy'), parts along dimension 0
- new_source_now: float32 [64, 32, 320], P(('shot', 'gx'), 'gy'), parts along dimension 0
- new_receiver_prev: float32 [64, 32, 320], P(('shot', 'gx'), 'gy'), parts along dimension 0
- new_receiver_now: float32 [64, 32, 320], P(('shot', 'gx'), 'gy'), parts along dimension 0
- snapshots: bfloat16 [8, 32, 32, 320], P('shot', 'gx', 'gy'), parts along dimension 0
- image: float32 [64, 32, 320], P(('shot', 'gx'), 'gy'), parts along dimension 0
The draws below stay inside these ranges and needn't reach their ends.
There are 2 independent parts, one for each index of `shot`. The reference program is written for one: setup_inputs(seed, part) draws one part's arguments, and reference() takes and returns one part's arrays. A program takes and returns all parts, laid end to end along the dimension named above; each array names one. Nothing has to cross between parts.
Inputs may be any that keep to these rules, and one draw needn't show every extreme that they name: `plan`: 4 different steps in increasing order; the first is 0 and the last is 9.
All inputs are finite; a program needn't handle non-finite values.
Results may differ from the reference program's by a relative error of at most 0.001.
Values sent between devices are 32-bit elements; how exact they have to be, the bound alone decides.
A program may use at most 64 MiB of HBM per device.

```python
import math
import jax
import jax.numpy as jnp
from jax import lax

NZ = 320
STEPS = 10
NSNAP = 4
NX = 32
NY = 32
NREC = 1024


def draw_plan(key, part):
    middle = jax.random.permutation(jax.random.fold_in(key, 11), STEPS - 2)[:NSNAP - 2] + 1
    middle = jnp.sort(middle.astype(jnp.int32))
    return jnp.concatenate([jnp.zeros((1,), jnp.int32), middle, jnp.full((1,), STEPS - 1, jnp.int32)])


def touch_ends(values, stream_key, least, largest):
    longest = values.shape.index(max(values.shape))
    spots = []
    for shift in (0, 1):
        where = [jax.random.randint(jax.random.fold_in(stream_key, axis), (), 0, length) for axis, length in enumerate(values.shape)]
        where[longest] = (where[longest] + shift) % values.shape[longest]
        spots.append(tuple(where))
    return values.at[spots[0]].set(least).at[spots[1]].set(largest)


def level_of(rng, shape, shards, low, high):
    level = 1.0
    for dim, blocks in shards:
        heights = jax.random.uniform(jax.random.fold_in(jax.random.fold_in(rng, 6), dim), (blocks,), jnp.float32, low / len(shards), high / len(shards))
        level = level * jnp.repeat(jnp.exp(heights), shape[dim] // blocks).reshape((-1,) + (1,) * (len(shape) - 1 - dim))
    return level


def normal_values(own_key, shape, deviation, most, cuts=(), kind=jnp.bfloat16):
    drawn = deviation * jax.random.normal(own_key, shape, jnp.float32)
    if cuts:
        drawn = drawn * level_of(own_key, shape, cuts, -0.22, 0.18)
    return jnp.clip(drawn, -most, most).astype(kind)


def setup_inputs(seed: int = 0, part: int = 0) -> dict:
    arg_keys = jax.random.split(jax.random.key(seed), 13)
    part_keys = jax.random.split(jax.random.fold_in(arg_keys[12], part), 13)
    source_prev = normal_values(part_keys[0], (NX, NY, NZ), 0.1, 0.6, ((0, 4), (1, 4)), jnp.float32)
    source_now = normal_values(part_keys[1], (NX, NY, NZ), 0.1, 0.6, ((0, 4), (1, 4)), jnp.float32)
    receiver_prev = normal_values(part_keys[2], (NX, NY, NZ), 1.0, 6.0, ((0, 4), (1, 4)), jnp.float32)
    receiver_now = normal_values(part_keys[3], (NX, NY, NZ), 1.0, 6.0, ((0, 4), (1, 4)), jnp.float32)
    speed_squared = jnp.clip(jnp.exp(math.log(0.18) - 1.2809339 * jax.random.uniform(part_keys[4], (NX, NY, NZ), jnp.float32) ** level_of(part_keys[4], (NX, NY, NZ), ((0, 4), (1, 4)), -0.2, 0.2)), 0.05, 0.18)
    wavelet = normal_values(part_keys[5], (STEPS,), 8.0, 40.0, (), jnp.float32)
    source_cell = jax.random.randint(part_keys[6], (1,), 0, NX * NY * NZ).astype(jnp.int32)
    traces = normal_values(part_keys[7], (STEPS, NREC), 3.0, 18.0, ((1, 16),), jnp.float32)
    receiver_cells = touch_ends(jax.random.randint(part_keys[8], (1, NREC), 0, NX * NY), jax.random.fold_in(part_keys[8], 1), 0, (NX * NY) - 1).astype(jnp.int32)
    plan = draw_plan(jax.random.fold_in(jax.random.fold_in(arg_keys[12], part), 71), part)
    stored_snapshots = normal_values(part_keys[10], (NSNAP, NX, NY, NZ), 1.0, 6.0, ((1, 4), (2, 4)))
    image_before = normal_values(part_keys[11], (NX, NY, NZ), 1.0, 6.0, ((0, 4), (1, 4)), jnp.float32)
    return {"source_prev": source_prev, "source_now": source_now, "receiver_prev": receiver_prev, "receiver_now": receiver_now, "speed_squared": speed_squared, "wavelet": wavelet, "source_cell": source_cell, "traces": traces, "receiver_cells": receiver_cells, "plan": plan, "stored_snapshots": stored_snapshots, "image_before": image_before}


STENCIL_COEFFS = (-205.0 / 72.0, 8.0 / 5.0, -1.0 / 5.0, 8.0 / 315.0, -1.0 / 560.0)


def stencil(padded):
    span_x = padded.shape[0] - 8
    span_y = padded.shape[1] - 8
    depth_cells = padded.shape[2]
    deepened = jnp.pad(padded, ((0, 0), (0, 0), (4, 4)))

    def window(shift_x, shift_y, shift_z):
        return deepened[4 + shift_x:4 + shift_x + span_x, 4 + shift_y:4 + shift_y + span_y,
                        4 + shift_z:4 + shift_z + depth_cells]

    summed = (3.0 * STENCIL_COEFFS[0]) * window(0, 0, 0)
    for distance in range(1, 5):
        neighbours = window(distance, 0, 0) + window(-distance, 0, 0)
        neighbours = neighbours + window(0, distance, 0) + window(0, -distance, 0)
        neighbours = neighbours + window(0, 0, distance) + window(0, 0, -distance)
        summed = summed + STENCIL_COEFFS[distance] * neighbours
    return summed


def reference(source_prev, source_now, receiver_prev, receiver_now, speed_squared, wavelet,
              source_cell, traces, receiver_cells, plan, stored_snapshots, image_before):
    grid_x, grid_y, depth_cells = source_now.shape
    total_steps = wavelet.shape[0]
    slot_count = plan.shape[0]
    cell_id = source_cell[0]
    site_x = cell_id // (grid_y * depth_cells)
    site_y = (cell_id // depth_cells) % grid_y
    site_z = cell_id % depth_cells
    previous, current = source_prev, source_now
    snapshots = jnp.zeros(stored_snapshots.shape, jnp.bfloat16)
    for step_index in range(total_steps):
        spread = stencil(jnp.pad(current, ((4, 4), (4, 4), (0, 0))))
        spread = spread.at[site_x, site_y, site_z].add(wavelet[step_index])
        latest = 2.0 * current - previous + speed_squared * spread
        previous, current = current, latest
        matches = plan == step_index
        snapshots = jnp.where(matches[:, None, None, None], current.astype(jnp.bfloat16)[None], snapshots)
    source_last, source_final = previous, current

    planes = jnp.zeros((total_steps, grid_x * grid_y), jnp.float32).at[:, receiver_cells[0]].add(traces)
    planes = planes.reshape(total_steps, grid_x, grid_y)
    previous, current = receiver_prev, receiver_now
    imaged = image_before
    for step_index in range(total_steps):
        back_time = total_steps - 1 - step_index
        spread = stencil(jnp.pad(current, ((4, 4), (4, 4), (0, 0))))
        spread = spread.at[:, :, 0].add(planes[back_time])
        latest = 2.0 * current - previous + speed_squared * spread
        previous, current = current, latest
        matches = plan == back_time
        slot_index = jnp.sum(jnp.where(matches, jnp.arange(slot_count, dtype=jnp.int32), 0)).astype(jnp.int32)
        present = jnp.any(matches)
        snapshot = lax.dynamic_index_in_dim(stored_snapshots, slot_index, 0, keepdims=False).astype(jnp.float32)
        imaged = imaged + jnp.where(present, snapshot * current, 0.0)
    return (source_last, source_final, previous, current, snapshots, imaged)
```

```python
import functools
import jax
import jax.numpy as jnp
from jax import lax
from jax.experimental import pallas as pl
from jax.experimental.pallas import tpu as pltpu
from jax.sharding import PartitionSpec as P

STENCIL_COEFFS = (-205.0 / 72.0, 8.0 / 5.0, -1.0 / 5.0, 8.0 / 315.0, -1.0 / 560.0)
LANES = 128
HALF = 4
LOW_X, HIGH_X, LOW_Y, HIGH_Y = range(4)
OPPOSITE = (HIGH_X, LOW_X, HIGH_Y, LOW_Y)
MESH = pl.DeviceIdType.MESH


def kernel(
    total_steps,
    source_prev,
    source_now,
    receiver_prev,
    receiver_now,
    speed_squared,
    wavelet,
    source_cell,
    traces,
    receiver_cells,
    plan,
    stored,
    image_before,
    out_source_prev,
    out_source_now,
    out_receiver_prev,
    out_receiver_now,
    out_snapshots,
    out_image,
    hist,
    speed,
    core,
    sides,
    packed,
    landed,
    records,
    gathered,
    planes,
    inject,
    send_sem,
    recv_sem,
    trace_send,
    trace_recv,
):
    block_x, block_y, depth = source_now.shape
    count_x, count_y = lax.axis_size("gx"), lax.axis_size("gy")
    me_x, me_y = lax.axis_index("gx"), lax.axis_index("gy")
    grid_y = block_y * count_y
    peers = count_x * count_y
    me = me_x * count_y + me_y
    width = speed.shape[2]
    full = depth // LANES
    own = traces.shape[1]
    slots = plan.shape[0]
    exists = (me_x > 0, me_x < count_x - 1, me_y > 0, me_y < count_y - 1)
    there = ({"gx": me_x - 1}, {"gx": me_x + 1}, {"gy": me_y - 1}, {"gy": me_y + 1})

    def peer_of(offset):
        other = lax.rem(me + offset, peers)
        return {"gx": other // count_y, "gy": lax.rem(other, count_y)}

    barrier = pltpu.get_barrier_semaphore()

    def greet(offset, carry):
        pl.semaphore_signal(barrier, inc=1, device_id=peer_of(offset), device_id_type=MESH)
        return carry

    for side in range(4):

        @pl.when(jnp.logical_not(exists[side]))
        def _():
            for field in range(2):
                for parity in range(2):
                    landed[field, parity, side] = jnp.zeros(landed.shape[3:], jnp.float32)

    lax.fori_loop(1, peers, greet, 0)

    row = lax.broadcasted_iota(jnp.int32, (block_y, width), 0)
    lane = lax.broadcasted_iota(jnp.int32, (block_y, width), 1)
    first_half = row < HALF
    tail_lane = lax.broadcasted_iota(jnp.int32, (block_y, LANES), 1)
    in_tail = tail_lane < LANES // 2

    records[...] = jnp.zeros_like(records)
    records[0:total_steps, :] = traces[...]
    records[total_steps : total_steps + 1, :] = receiver_cells[...].astype(jnp.float32)
    for field, (before, now) in enumerate(
        ((source_prev, source_now), (receiver_prev, receiver_now))
    ):
        for index, array in enumerate((before, now)):
            hist[field, index, HALF : HALF + block_x, :, full * LANES :] = jnp.zeros(
                (block_x, block_y, width - full * LANES), jnp.float32
            )
            hist[field, index, HALF : HALF + block_x, :, 0:depth] = array[...]

    def halo_copy(field, parity, side):
        return pltpu.make_async_remote_copy(
            src_ref=packed.at[field, side],
            dst_ref=landed.at[field, parity, OPPOSITE[side]],
            send_sem=send_sem.at[field, side],
            recv_sem=recv_sem.at[field, parity, OPPOSITE[side]],
            device_id=there[side],
            device_id_type=MESH,
        )

    def arrival(field, parity, side):
        return pltpu.make_async_remote_copy(
            src_ref=packed.at[field, side],
            dst_ref=landed.at[field, parity, side],
            send_sem=send_sem.at[field, side],
            recv_sem=recv_sem.at[field, parity, side],
            device_id=there[side],
            device_id_type=MESH,
        )

    def pack(field, side, tiles):
        for i in range(HALF):
            for j in range(full):
                packed[field, side, i * full + j] = tiles[i][:, j * LANES : (j + 1) * LANES]
        tails = [tile[:, full * LANES :] for tile in tiles]
        for i in range(2):
            packed[field, side, HALF * full + i] = tails[i] + pltpu.roll(
                tails[i + 2], LANES // 2, axis=1
            )

    def unpack(field, parity, side):
        tails = []
        for i in range(2):
            both = landed[field, parity, side, HALF * full + i]
            tails.append((both, pltpu.roll(both, LANES // 2, axis=1)))
        result = []
        for i in range(HALF):
            tail = jnp.where(in_tail, tails[i % 2][i // 2], 0.0)
            result.append(
                jnp.concatenate(
                    [landed[field, parity, side, i * full + j] for j in range(full)] + [tail],
                    axis=1,
                )
            )
        return result

    def send(field, index, parity):
        tiles = [hist[field, index, HALF + x] for x in range(block_x)]
        pack(field, LOW_X, tiles[:HALF])
        pack(field, HIGH_X, tiles[block_x - HALF :])
        turned = [pltpu.roll(tiles[i + HALF], HALF, axis=0) for i in range(HALF)]
        pack(field, LOW_Y, [jnp.where(first_half, tiles[i], turned[i]) for i in range(HALF)])
        pack(field, HIGH_Y, [jnp.where(first_half, turned[i], tiles[i]) for i in range(HALF)])
        for side in range(4):

            @pl.when(exists[side])
            def _():
                halo_copy(field, parity, side).start()

    def receive(field, index, parity):
        for side in range(4):

            @pl.when(exists[side])
            def _():
                arrival(field, parity, side).wait()

        low, high = unpack(field, parity, LOW_X), unpack(field, parity, HIGH_X)
        for i in range(HALF):
            hist[field, index, i] = low[i]
            hist[field, index, HALF + block_x + i] = high[i]
        low, high = unpack(field, parity, LOW_Y), unpack(field, parity, HIGH_Y)
        for i in range(HALF):
            sides[field, i] = jnp.where(first_half, high[i], low[i])
            sides[field, i + HALF] = pltpu.roll(
                jnp.where(first_half, low[i], high[i]), HALF, axis=0
            )

    def advance(field, index, extra):
        for x in range(block_x):
            center = hist[field, index, HALF + x]
            side = sides[field, x]
            spread = 3.0 * STENCIL_COEFFS[0] * center
            for k in range(1, HALF + 1):
                around = hist[field, index, HALF + x - k] + hist[field, index, HALF + x + k]
                around += pltpu.roll(center, k, axis=1) + pltpu.roll(center, width - k, axis=1)
                around += pltpu.roll(jnp.where(row < block_y - k, center, side), k, axis=0)
                around += pltpu.roll(jnp.where(row < k, side, center), block_y - k, axis=0)
                spread += STENCIL_COEFFS[k] * around
            latest = 2.0 * center - hist[field, index - 1, HALF + x] + speed[x] * spread
            hist[field, index + 1, HALF + x] = extra(x, latest)

    pl.semaphore_wait(barrier, peers - 1)
    send(0, 1, 0)
    send(1, 1, 0)

    def trace_copy(offset):
        return pltpu.make_async_remote_copy(
            src_ref=records,
            dst_ref=gathered.at[offset - 1],
            send_sem=trace_send,
            recv_sem=trace_recv,
            device_id=peer_of(offset),
            device_id_type=MESH,
        )

    def spread_records(offset, carry):
        trace_copy(offset).start()
        return carry

    lax.fori_loop(1, peers, spread_records, 0)

    speed[:, :, full * LANES :] = jnp.zeros(
        (block_x, block_y, width - full * LANES), jnp.float32
    )
    speed[:, :, 0:depth] = speed_squared[...]
    for x in range(block_x):
        flat = ((me_x * block_x + x) * grid_y + me_y * block_y + row) * depth + lane
        hit = (flat == source_cell[0]) & (lane < depth)
        core[x] = jnp.where(hit, speed[x], 0.0)

    def source_extra(step):
        return lambda x, latest: latest + wavelet[step] * core[x]

    def receiver_extra(step):
        back = total_steps - 1 - step

        def add(x, latest):
            return jnp.concatenate(
                [latest[:, :LANES] + inject[back, x], latest[:, LANES:]], axis=1
            )

        return add

    def collect_planes():
        everything = pltpu.make_async_remote_copy(
            src_ref=gathered.at[pl.ds(0, peers - 1)],
            dst_ref=gathered.at[pl.ds(0, peers - 1)],
            send_sem=trace_send,
            recv_sem=trace_recv,
            device_id=there[0],
            device_id_type=MESH,
        )
        everything.wait()
        gathered[peers - 1] = records[...]
        cells = block_x * block_y
        number = lax.broadcasted_iota(jnp.int32, (cells, own), 0)
        number = (me_x * block_x + number // block_y) * grid_y + me_y * block_y + number % block_y
        number = number.astype(jnp.float32)

        def one(slot):
            block = gathered[slot]
            chosen = (block[total_steps : total_steps + 1, :] == number).astype(jnp.float32)
            return lax.dot_general(
                chosen,
                block,
                (((1,), (1,)), ((), ())),
                precision=lax.Precision.HIGHEST,
                preferred_element_type=jnp.float32,
            )

        group = 16 if peers % 16 == 0 else 1

        def several(index, total):
            for j in range(group):
                total = total + one(index * group + j)
            return total

        total = lax.fori_loop(
            0, peers // group, several, jnp.zeros((cells, records.shape[0]), jnp.float32)
        )
        planes[...] = jnp.zeros_like(planes)
        planes[:, 0 : records.shape[0]] = total
        for x in range(block_x):
            rows = planes[x * block_y : (x + 1) * block_y, :]
            for step in range(total_steps):
                turned = pltpu.roll(rows, (LANES - step) % LANES, axis=1) if step else rows
                inject[step, x] = jnp.where(tail_lane == 0, turned * speed[x, :, :LANES], 0.0)

    def both(step, carry):
        parity = lax.rem(step, 2)
        for field, extra in enumerate((source_extra, receiver_extra)):
            receive(field, step + 1, parity)
            if field == 1:
                pl.when(step == 0)(collect_planes)
            advance(field, step + 1, extra(step))

            @pl.when(step < total_steps - 1)
            def _():
                send(field, step + 2, 1 - parity)

        return carry

    lax.fori_loop(0, total_steps, both, 0)
    inner = slice(HALF, HALF + block_x)
    out_source_prev[...] = hist[0, total_steps, inner, :, 0:depth]
    out_source_now[...] = hist[0, total_steps + 1, inner, :, 0:depth]
    out_receiver_prev[...] = hist[1, total_steps, inner, :, 0:depth]
    out_receiver_now[...] = hist[1, total_steps + 1, inner, :, 0:depth]
    total = image_before[...]
    for slot in range(slots):
        taken = hist[0, plan[slot] + 2]
        out_snapshots[slot] = taken[inner, :, 0:depth].astype(jnp.bfloat16)
        taken = hist[1, total_steps + 1 - plan[slot]]
        total = total + stored[slot].astype(jnp.float32) * taken[inner, :, 0:depth]
    out_image[...] = total


def body(*arrays):
    source_now, wavelet, traces, stored, plan = (arrays[i] for i in (1, 5, 7, 10, 9))
    block_x, block_y, depth = source_now.shape
    total_steps = wavelet.shape[0]
    own = traces.shape[1]
    peers = lax.axis_size("gx") * lax.axis_size("gy")
    width = -(-depth // LANES) * LANES
    record_rows = -(-(total_steps + 1) // 8) * 8
    tiles = HALF * depth // LANES
    vmem = pl.BlockSpec(memory_space=pltpu.VMEM)
    smem = pl.BlockSpec(memory_space=pltpu.SMEM)
    field = jax.ShapeDtypeStruct(source_now.shape, jnp.float32)
    f32 = jnp.float32
    return pl.pallas_call(
        functools.partial(kernel, total_steps),
        out_shape=(
            field,
            field,
            field,
            field,
            jax.ShapeDtypeStruct(stored.shape, jnp.bfloat16),
            field,
        ),
        in_specs=[vmem] * 5 + [smem, smem, vmem, vmem, smem, vmem, vmem],
        out_specs=[vmem] * 6,
        scratch_shapes=[
            pltpu.VMEM((2, total_steps + 2, block_x + 2 * HALF, block_y, width), f32),
            pltpu.VMEM((block_x, block_y, width), f32),
            pltpu.VMEM((block_x, block_y, width), f32),
            pltpu.VMEM((2, block_x, block_y, width), f32),
            pltpu.VMEM((2, 4, tiles, block_y, LANES), f32),
            pltpu.VMEM((2, 2, 4, tiles, block_y, LANES), f32),
            pltpu.VMEM((record_rows, own), f32),
            pltpu.VMEM((peers, record_rows, own), f32),
            pltpu.VMEM((block_x * block_y, LANES), f32),
            pltpu.VMEM((total_steps, block_x, block_y, LANES), f32),
            pltpu.SemaphoreType.DMA((2, 4)),
            pltpu.SemaphoreType.DMA((2, 2, 4)),
            pltpu.SemaphoreType.DMA,
            pltpu.SemaphoreType.DMA,
        ],
        compiler_params=pltpu.CompilerParams(collective_id=0, has_side_effects=True),
    )(*arrays)


def solution(mesh):
    block = P(("shot", "gx"), "gy", None)
    kept = P("shot", "gx", "gy", None)
    return jax.shard_map(
        body,
        mesh=mesh,
        in_specs=(
            block,
            block,
            block,
            block,
            block,
            P("shot"),
            P("shot"),
            P("shot", ("gx", "gy")),
            P("shot", ("gx", "gy")),
            P("shot"),
            kept,
            block,
        ),
        out_specs=(block, block, block, block, kept, block),
        check_vma=False,
    )
```
